512 devices in a mesh: section: 32 (over z, core), sp: 16 (over x, y).
Axes of the slice: x: 4, y: 4, z: 16, core: 2. Of those that a mesh axis runs over, the one named last changes fastest.
Arguments:
- query: bfloat16 [32, 2048, 8192], P('section', 'sp'), may hold values from -11 to 11
- keyval: bfloat16 [32, 2048, 2048], P('section', 'sp'), may hold values from -11 to 11
- cache: bfloat16 [32, 16, 256, 256], P('section', 'sp'), may hold values from -4 to 4, as said below
- offsets: int32 [32], P('section'), may hold values from 0 to 32767
- lengths: int32 [32], P('section'), may hold values from 1 to 256
Outputs:
- forwarded: bfloat16 [32, 2048, 8192], P('section', 'sp')
The draws below stay inside these ranges and needn't reach their ends.
Inputs may be any that keep to these rules, and one draw needn't show every extreme that they name: `cache`: slot k holds key-value head k * 8 // 16; slots that hold the same head are equal.
All inputs are finite; a program needn't handle non-finite values.
Results may differ from the reference program's by a relative error of at most 0.0096.
Values may be sent and summed in bfloat16 or wider, within the bound.
A program may use at most 64 MiB of HBM per device.

```python
import math
import jax
import jax.numpy as jnp
from jax import lax

QUERY_HEADS = 64
KEY_VALUE_HEADS = 8
HEAD_SIZE = 128
CACHE_POSITIONS = 256
RELAY_SECTIONS = 32
PREFILL_TOKENS = 2048
KEY_VALUE_SLOTS = 16
BLOCK = 512


def draw_query(key, part):
    section_key = jax.random.fold_in(key, 11)
    value_entries = jnp.clip(jax.random.normal(section_key, (RELAY_SECTIONS, PREFILL_TOKENS, QUERY_HEADS, HEAD_SIZE), jnp.float32), -4.0, 4.0)
    return value_entries.reshape(RELAY_SECTIONS, PREFILL_TOKENS, QUERY_HEADS * HEAD_SIZE).astype(jnp.bfloat16)


def draw_keyval(key, part):
    section_key = jax.random.fold_in(key, 22)
    value_entries = jnp.clip(jax.random.normal(section_key, (RELAY_SECTIONS, PREFILL_TOKENS, KEY_VALUE_HEADS, 2 * HEAD_SIZE), jnp.float32), -4.0, 4.0)
    return value_entries.reshape(RELAY_SECTIONS, PREFILL_TOKENS, KEY_VALUE_HEADS * 2 * HEAD_SIZE).astype(jnp.bfloat16)


def draw_cache(key, part):
    section_key = jax.random.fold_in(key, 33)
    head_list = jnp.clip(jax.random.normal(section_key, (RELAY_SECTIONS, KEY_VALUE_HEADS, CACHE_POSITIONS, 2 * HEAD_SIZE), jnp.float32), -4.0, 4.0)
    owner_section = jnp.arange(KEY_VALUE_SLOTS, dtype=jnp.int32) * KEY_VALUE_HEADS // KEY_VALUE_SLOTS
    return jnp.take(head_list, owner_section, axis=1).astype(jnp.bfloat16)


def touch_ends(entries, rng, least, top_value):
    dims = entries.shape
    spot = [jax.random.randint(jax.random.fold_in(rng, axis), (), 0, dims[axis]) for axis in range(len(dims))]
    entries = entries.at[tuple(spot)].set(least)
    longest = dims.index(max(dims))
    spot[longest] = (spot[longest] + 1) % dims[longest]
    return entries.at[tuple(spot)].set(top_value)


def setup_inputs(seed: int = 0) -> dict:
    seeds = jax.random.split(jax.random.key(seed), 6)
    query = draw_query(jax.random.fold_in(seeds[5], 71), 0)
    keyval = draw_keyval(jax.random.fold_in(seeds[5], 71), 0)
    cache = draw_cache(jax.random.fold_in(seeds[5], 71), 0)
    offsets = touch_ends(jax.random.randint(seeds[3], (RELAY_SECTIONS,), 0, 16 * PREFILL_TOKENS), jax.random.fold_in(seeds[3], 1), 0, (16 * PREFILL_TOKENS) - 1).astype(jnp.int32)
    lengths = touch_ends(jax.random.randint(seeds[4], (RELAY_SECTIONS,), 1, CACHE_POSITIONS + 1), jax.random.fold_in(seeds[4], 1), 1, CACHE_POSITIONS).astype(jnp.int32)
    return {"query": query, "keyval": keyval, "cache": cache, "offsets": offsets, "lengths": lengths}


ROPE_BASE = 500000.0

def rotation_tables(positions, head_width):
    half_width = head_width // 2
    exponent = jnp.arange(half_width, dtype=jnp.float32) * (-2.0 / head_width)
    frequency = jnp.power(jnp.float32(ROPE_BASE), exponent)
    angle = positions.astype(jnp.float32)[:, None] * frequency[None, :]
    return (jnp.cos(angle), jnp.sin(angle))

def rotate_pair(value_entries, cosine, sine):
    half_width = value_entries.shape[-1] // 2
    first = value_entries[..., :half_width].astype(jnp.float32)
    second = value_entries[..., half_width:].astype(jnp.float32)
    cos_wide = cosine[:, None, :]
    sin_wide = sine[:, None, :]
    return jnp.concatenate([first * cos_wide - second * sin_wide, second * cos_wide + first * sin_wide], axis=-1)

def attend_head(query_rows, key_rows, value_rows, cache_keys, cache_values, length, block_rows):
    scale = 1.0 / math.sqrt(query_rows.shape[-1])
    contract = (((1,), (1,)), ((), ()))
    cache_live = jnp.arange(cache_keys.shape[0], dtype=jnp.int32) < length
    results = []
    for block_index in range(query_rows.shape[0] // block_rows):
        first_row = block_index * block_rows
        key_reach = first_row + block_rows
        block_queries = query_rows[first_row:key_reach]
        cache_scores = lax.dot_general(block_queries, cache_keys, contract, preferred_element_type=jnp.float32) * scale
        own_scores = lax.dot_general(block_queries, key_rows[:key_reach], contract, preferred_element_type=jnp.float32) * scale
        cache_scores = jnp.where(cache_live[None, :], cache_scores, -jnp.inf)
        row_place = first_row + jnp.arange(block_rows, dtype=jnp.int32)
        causal = jnp.arange(key_reach, dtype=jnp.int32)[None, :] <= row_place[:, None]
        own_scores = jnp.where(causal, own_scores, -jnp.inf)
        row_top = jnp.maximum(lax.optimization_barrier(jnp.max(cache_scores, axis=1)), lax.optimization_barrier(jnp.max(own_scores, axis=1)))
        cache_weights = jnp.exp(cache_scores - row_top[:, None])
        own_weights = jnp.exp(own_scores - row_top[:, None])
        row_total = lax.optimization_barrier(jnp.sum(cache_weights, axis=1)) + lax.optimization_barrier(jnp.sum(own_weights, axis=1))
        numerator = jnp.dot(cache_weights.astype(jnp.bfloat16), cache_values, preferred_element_type=jnp.float32)
        numerator = numerator + jnp.dot(own_weights.astype(jnp.bfloat16), value_rows[:key_reach], preferred_element_type=jnp.float32)
        results.append((numerator / row_total[:, None]).astype(jnp.bfloat16))
    return jnp.concatenate(results, axis=0)

def reference(query, keyval, cache, offsets, lengths):
    group_width = QUERY_HEADS // KEY_VALUE_HEADS

    def one_section(items):
        section_query, section_key_value, section_cache, section_offset, section_length = items
        positions = section_offset + jnp.arange(PREFILL_TOKENS, dtype=jnp.int32)
        cosine, sine = rotation_tables(positions, HEAD_SIZE)
        rotated_queries = rotate_pair(section_query.reshape(PREFILL_TOKENS, QUERY_HEADS, HEAD_SIZE), cosine, sine).astype(jnp.bfloat16)
        pair_matched = section_key_value.reshape(PREFILL_TOKENS, KEY_VALUE_HEADS, 2 * HEAD_SIZE)
        rotated_keys = rotate_pair(pair_matched[..., :HEAD_SIZE], cosine, sine).astype(jnp.bfloat16)
        plain_values = pair_matched[..., HEAD_SIZE:]

        def one_head(head_index):
            group_index = head_index // group_width
            slot_index = head_index * KEY_VALUE_SLOTS // QUERY_HEADS
            head_queries = lax.dynamic_index_in_dim(rotated_queries, head_index, 1, False)
            head_keys = lax.dynamic_index_in_dim(rotated_keys, group_index, 1, False)
            head_values = lax.dynamic_index_in_dim(plain_values, group_index, 1, False)
            slot_cache = lax.dynamic_index_in_dim(section_cache, slot_index, 0, False)
            return attend_head(head_queries, head_keys, head_values, slot_cache[:, :HEAD_SIZE], slot_cache[:, HEAD_SIZE:], section_length, BLOCK)
        head_list = lax.map(one_head, jnp.arange(QUERY_HEADS, dtype=jnp.int32))
        return jnp.transpose(head_list, (1, 0, 2)).reshape(PREFILL_TOKENS, QUERY_HEADS * HEAD_SIZE)
    attended = lax.map(one_section, (query, keyval, cache, offsets, lengths))
    return jnp.roll(attended, 1, axis=0)
```

```python
import functools
import math

import jax
import jax.numpy as jnp
from jax import lax
from jax.experimental import pallas as pl
from jax.experimental.pallas import tpu as pltpu
from jax.sharding import PartitionSpec as P

HEAD = 128
ROWS = 128
SIDE = 4
CACHE = 256
TILE = 512
SPAN = SIDE * SIDE * ROWS
ROPE_BASE = 500000.0
NEG = -1e30
SCALE = math.log2(math.e) / math.sqrt(HEAD)
MESH = pl.DeviceIdType.MESH
CONTRACT = (((1,), (1,)), ((), ()))
ORDER = (1, 3, 2)


def place(family, a, t):
    return SIDE * a + t if family == 0 else SIDE * t + a


def head_of(family, a):
    return 2 * a + 1 - a // 2 if family == 0 else 2 * a + a // 2


def kernel(
    sections,
    length_ref,
    query,
    keyval,
    cache,
    block_tab,
    row_tab,
    out,
    kvland,
    qland,
    cland,
    keys,
    values,
    qa,
    qb,
    sa,
    sb,
    ma,
    mb,
    obuf,
    kv1_send,
    kv2_send,
    kv_recv,
    q_send,
    q_recv,
    c_send,
    c_recv,
    o_send,
    o_recv,
):
    s = lax.axis_index("section")
    d = lax.axis_index("sp")
    x = d // SIDE
    y = d % SIDE
    head_at = (x, y)
    row_at = (y, x)
    after = lax.rem(s + 1, sections)
    before = lax.rem(s + sections - 1, sections)

    barrier = pltpu.get_barrier_semaphore()
    peers = []
    for k in range(1, SIDE):
        for f in range(2):
            peers.append((s, place(f, lax.rem(head_at[f] + k, SIDE), row_at[f])))
    for section in (after, before):
        peers.append((section, d))
        for k in range(1, SIDE):
            for f in range(2):
                peers.append((section, place(f, lax.rem(head_at[f] + k, SIDE), row_at[f])))
    for peer in peers:
        pl.semaphore_signal(barrier, inc=1, device_id=peer, device_id_type=MESH)
    pl.semaphore_wait(barrier, len(peers))

    def remote(source, target, send, recv, section, device):
        return pltpu.make_async_remote_copy(
            src_ref=source,
            dst_ref=target,
            send_sem=send,
            recv_sem=recv,
            device_id=(section, device),
            device_id_type=MESH,
        )

    def kv_part(f, a):
        return keyval.at[:, pl.ds(pl.multiple_of(head_of(f, a) * 256, 256), 256)]

    def q_part(f, a, half):
        return query.at[:, pl.ds(pl.multiple_of(head_of(f, a) * 1024 + half * 512, 512), 512)]

    def kv1(f, k):
        a = lax.rem(head_at[f] + k, SIDE)
        return remote(
            kv_part(f, a), kvland.at[f, d], kv1_send.at[f, k - 1], kv_recv.at[f, d], s, place(f, a, row_at[f])
        )

    def kv2(f, j, k):
        block = place(f, lax.rem(head_at[f] + j, SIDE), row_at[f])
        source = kv_part(f, head_at[f]) if j == 0 else kvland.at[f, block]
        target = place(f, head_at[f], lax.rem(row_at[f] + k, SIDE))
        return remote(source, kvland.at[f, block], kv2_send.at[f, j, k - 1], kv_recv.at[f, block], s, target)

    def q_copy(f, k, half):
        a = lax.rem(head_at[f] + k, SIDE)
        return remote(
            q_part(f, a, half),
            qland.at[f, head_at[f], half],
            q_send.at[f, k - 1, half],
            q_recv.at[f, head_at[f], half],
            s,
            place(f, a, row_at[f]),
        )

    def kv_own(f):
        return pltpu.make_async_copy(kv_part(f, head_at[f]), kvland.at[f, d], kv_recv.at[f, d])

    def q_own(f, half):
        return pltpu.make_async_copy(
            q_part(f, head_at[f], half), qland.at[f, head_at[f], half], q_recv.at[f, head_at[f], half]
        )

    def q_wait(f, a, half):
        pltpu.make_async_copy(q_part(f, a, half), qland.at[f, a, half], q_recv.at[f, a, half]).wait()

    def kv_wait(f, block):
        pltpu.make_async_copy(kv_part(f, 0), kvland.at[f, block], kv_recv.at[f, block]).wait()

    def cache_own(f):
        return pltpu.make_async_copy(cache, cland.at[f], c_recv.at[f])

    def cache_copy(f, k):
        if f == 0:
            target = SIDE * x + SIDE - 1 - y
        else:
            target = SIDE * lax.rem(x + k, SIDE) + y
        return remote(cache, cland.at[f], c_send.at[f, k - 1], c_recv.at[f], s, target)

    holds = (x // 2 != y // 2, x == y)

    def out_copy(f, a, half):
        column = head_of(f, head_at[f]) * 1024 + half * 512
        return remote(
            obuf.at[f, a, half],
            out.at[:, pl.ds(pl.multiple_of(column, 512), 512)],
            o_send.at[f, a, half],
            o_recv.at[f, head_at[f], half],
            after,
            place(f, a, row_at[f]),
        )

    def out_wait(f, a, half):
        column = head_of(f, a) * 1024 + half * 512
        pltpu.make_async_copy(
            obuf.at[f, a, half], out.at[:, pl.ds(pl.multiple_of(column, 512), 512)], o_recv.at[f, a, half]
        ).wait()

    for k in ORDER:
        for f in range(2):
            kv1(f, k).start()
    for k in ORDER:
        for f in range(2):
            kv2(f, 0, k).start()
    for f in range(2):
        kv_own(f).start()
        for half in range(2):
            q_own(f, half).start()

    for f, ks in ((0, (1,)), (1, ORDER)):

        @pl.when(holds[f])
        def _():
            cache_own(f).start()
            for k in ks:
                cache_copy(f, k).start()

    for half in range(2):
        for k in ORDER:
            q_copy(0, k, half).start()

    values[:, :, HEAD:] = jnp.ones((2, CACHE + SPAN, HEAD), jnp.bfloat16)

    for j in ORDER:
        kv_wait(0, place(0, lax.rem(head_at[0] + j, SIDE), row_at[0]))
        for k in ORDER:
            kv2(0, j, k).start()
    for j in ORDER:
        kv_wait(1, place(1, lax.rem(head_at[1] + j, SIDE), row_at[1]))
        for k in ORDER:
            kv2(1, j, k).start()
    for half in range(2):
        for k in ORDER:
            q_copy(1, k, half).start()
    for f in range(2):
        kv_wait(f, d)

    def tables(block):
        cos_block = block_tab[0, block]
        sin_block = block_tab[1, block]
        cos_signed = block_tab[2, block]
        sin_signed = block_tab[3, block]
        cos_row = row_tab[0]
        sin_row = row_tab[1]
        cosine = cos_block * cos_row - sin_block * sin_row
        sine = sin_signed * cos_row + cos_signed * sin_row
        return cosine, sine

    def rotate(entries, cosine, sine):
        wide = entries.astype(jnp.float32)
        return wide * cosine + pltpu.roll(wide, HEAD // 2, 1) * sine

    def take_block(f, block):
        cosine, sine = tables(block)
        first = pl.multiple_of(CACHE + block * ROWS, ROWS)
        keys[f, pl.ds(first, ROWS), :] = rotate(kvland[f, block, :, :HEAD], cosine, sine).astype(jnp.bfloat16)
        values[f, pl.ds(first, ROWS), :HEAD] = kvland[f, block, :, HEAD:]

    def take_cache(f):
        cache_own(f).wait()
        keys[f, :CACHE, :] = cland[f, :, :HEAD]
        values[f, :CACHE, :HEAD] = cland[f, :, HEAD:]

    def take_query(f, a, half, target):
        q_wait(f, a, half)
        cosine, sine = tables(place(f, a, row_at[f]))
        for h in range(TILE // ROWS):
            head = qland[f, a, half, :, h * HEAD : (h + 1) * HEAD]
            target[h * ROWS : (h + 1) * ROWS, :] = (rotate(head, cosine, sine) * SCALE).astype(jnp.bfloat16)

    length = length_ref[0]

    def score(f, q_ref, reach, shift, s_ref, m_ref):
        q = q_ref[...]
        column = lax.broadcasted_iota(jnp.int32, (1, CACHE), 1)
        part = lax.dot_general(q, keys[f, :CACHE, :], CONTRACT, preferred_element_type=jnp.float32)
        part = jnp.where(column < length, part, NEG)
        s_ref[:, :CACHE] = part
        top = jnp.maximum(part[:, :128], part[:, 128:])
        if reach > 512:
            part = lax.dot_general(
                q, keys[f, CACHE : reach - 256, :], CONTRACT, preferred_element_type=jnp.float32
            )
            s_ref[:, CACHE : reach - 256] = part
            for c in range(0, reach - 512, 128):
                top = jnp.maximum(top, part[:, c : c + 128])
        part = lax.dot_general(
            q, keys[f, reach - 256 : reach + 256, :], CONTRACT, preferred_element_type=jnp.float32
        )
        column = lax.broadcasted_iota(jnp.int32, (1, 512), 1)
        row = lax.rem(lax.broadcasted_iota(jnp.int32, (TILE, 1), 0), ROWS) + shift
        part = jnp.where(column <= row, part, NEG)
        s_ref[:, reach - 256 : reach + 256] = part
        for c in range(0, 512, 128):
            top = jnp.maximum(top, part[:, c : c + 128])
        m_ref[...] = jnp.broadcast_to(jnp.max(top, axis=1, keepdims=True), (TILE, 128))

    def combine(f, a, half, reach, s_ref, m_ref):
        width = reach + CACHE
        top = jnp.concatenate([m_ref[...]] * (width // 128), axis=1)
        probs = jnp.exp2(s_ref[:, :width] - top).astype(jnp.bfloat16)
        mixed = jnp.dot(probs, values[f, :width, :], preferred_element_type=jnp.float32)
        result = (mixed[:, :HEAD] / mixed[:, HEAD:]).astype(jnp.bfloat16)
        for h in range(TILE // ROWS):
            obuf[f, a, half, :, h * HEAD : (h + 1) * HEAD] = result[h * ROWS : (h + 1) * ROWS, :]

    def prepare(i):
        for k in ORDER:
            kv_wait(0, place(0, i, lax.rem(row_at[0] + k, SIDE)))
        for j in range(SIDE):
            take_block(0, SIDE * i + j)

    shift = row_at[0] * ROWS
    take_cache(0)
    prepare(0)
    take_query(0, 0, 0, qa)
    score(0, qa, 512, shift, sa, ma)
    for i in range(SIDE):
        reach = 512 * (i + 1)
        take_query(0, i, 1, qb)
        score(0, qb, reach, shift, sb, mb)
        combine(0, i, 0, reach, sa, ma)
        if i > 0:
            out_copy(0, i - 1, 1).start()
        if i < SIDE - 1:
            prepare(i + 1)
            take_query(0, i + 1, 0, qa)
            score(0, qa, reach + 512, shift, sa, ma)
        combine(0, i, 1, reach, sb, mb)
        out_copy(0, i, 0).start()

    take_cache(1)
    for k in ORDER:

        def wait_block(a, carry, k=k):
            kv_wait(1, place(1, a, lax.rem(row_at[1] + k, SIDE)))
            return carry

        lax.fori_loop(0, SIDE, wait_block, 0)

    def take_one(block, carry):
        take_block(1, block)
        return carry

    lax.fori_loop(0, SIDE * SIDE, take_one, 0)
    out_copy(0, SIDE - 1, 1).start()

    def run(reach):
        take_query(1, 0, 0, qa)
        score(1, qa, reach, 0, sa, ma)

        def unit(a, carry):
            take_query(1, a, 1, qb)
            score(1, qb, reach, a * ROWS, sb, mb)
            combine(1, a, 0, reach, sa, ma)

            @pl.when(a > 0)
            def _():
                out_copy(1, a - 1, 1).start()

            @pl.when(a < SIDE - 1)
            def _():
                take_query(1, a + 1, 0, qa)

            score(1, qa, reach, (a + 1) * ROWS, sa, ma)
            combine(1, a, 1, reach, sb, mb)
            out_copy(1, a, 0).start()
            return carry

        lax.fori_loop(0, SIDE, unit, 0)

    for t in range(SIDE):

        @pl.when(row_at[1] == t)
        def _(t=t):
            run(512 * (t + 1))

    out_copy(1, SIDE - 1, 1).start()

    for f in range(2):
        for k in ORDER:
            kv1(f, k).wait_send()
            for j in range(SIDE):
                kv2(f, j, k).wait_send()
            for half in range(2):
                q_copy(f, k, half).wait_send()
    for f, ks in ((0, (1,)), (1, ORDER)):

        @pl.when(holds[f])
        def _():
            for k in ks:
                cache_copy(f, k).wait_send()

    for f in range(2):
        for a in range(SIDE):
            for half in range(2):
                out_copy(f, a, half).wait_send()
                out_wait(f, a, half)


def angles(positions):
    exponent = jnp.arange(HEAD // 2, dtype=jnp.float32) * (-2.0 / HEAD)
    frequency = jnp.power(jnp.float32(ROPE_BASE), exponent)
    angle = positions.astype(jnp.float32)[:, None] * frequency[None, :]
    return jnp.cos(angle), jnp.sin(angle)


def on_device(query, keyval, cache, offsets, lengths):
    sections = lax.axis_size("section")
    blocks = offsets[0] + ROWS * jnp.arange(SIDE * SIDE, dtype=jnp.int32)
    cos_block, sin_block = angles(blocks)
    cos_row, sin_row = angles(jnp.arange(ROWS, dtype=jnp.int32))
    block_tab = jnp.stack(
        [
            jnp.concatenate([cos_block, cos_block], axis=1),
            jnp.concatenate([sin_block, sin_block], axis=1),
            jnp.concatenate([-cos_block, cos_block], axis=1),
            jnp.concatenate([-sin_block, sin_block], axis=1),
        ]
    )[:, :, None, :]
    row_tab = jnp.stack(
        [
            jnp.concatenate([cos_row, cos_row], axis=1),
            jnp.concatenate([sin_row, sin_row], axis=1),
        ]
    )
    bf16 = jnp.bfloat16
    anywhere = pl.BlockSpec(memory_space=pl.ANY)
    vmem = pl.BlockSpec(memory_space=pltpu.VMEM)
    result = pl.pallas_call(
        functools.partial(kernel, sections),
        out_shape=jax.ShapeDtypeStruct((ROWS, 64 * HEAD), bf16),
        in_specs=[pl.BlockSpec(memory_space=pltpu.SMEM), anywhere, anywhere, anywhere, vmem, vmem],
        out_specs=anywhere,
        scratch_shapes=[
            pltpu.VMEM((2, SIDE * SIDE, ROWS, 2 * HEAD), bf16),
            pltpu.VMEM((2, SIDE, 2, ROWS, TILE), bf16),
            pltpu.VMEM((2, CACHE, 2 * HEAD), bf16),
            pltpu.VMEM((2, CACHE + SPAN, HEAD), bf16),
            pltpu.VMEM((2, CACHE + SPAN, 2 * HEAD), bf16),
            pltpu.VMEM((TILE, HEAD), bf16),
            pltpu.VMEM((TILE, HEAD), bf16),
            pltpu.VMEM((TILE, CACHE + SPAN), jnp.float32),
            pltpu.VMEM((TILE, CACHE + SPAN), jnp.float32),
            pltpu.VMEM((TILE, 128), jnp.float32),
            pltpu.VMEM((TILE, 128), jnp.float32),
            pltpu.VMEM((2, SIDE, 2, ROWS, TILE), bf16),
            pltpu.SemaphoreType.DMA((2, 3)),
            pltpu.SemaphoreType.DMA((2, SIDE, 3)),
            pltpu.SemaphoreType.DMA((2, SIDE * SIDE)),
            pltpu.SemaphoreType.DMA((2, 3, 2)),
            pltpu.SemaphoreType.DMA((2, SIDE, 2)),
            pltpu.SemaphoreType.DMA((2, 3)),
            pltpu.SemaphoreType.DMA((2,)),
            pltpu.SemaphoreType.DMA((2, SIDE, 2)),
            pltpu.SemaphoreType.DMA((2, SIDE, 2)),
        ],
        compiler_params=pltpu.CompilerParams(
            collective_id=0, has_side_effects=True, vmem_limit_bytes=48 << 20
        ),
    )(lengths, query[0], keyval[0], cache[0, 0], block_tab, row_tab)
    return result[None]


def solution(mesh):
    return jax.shard_map(
        on_device,
        mesh=mesh,
        in_specs=(
            P("section", "sp", None),
            P("section", "sp", None),
            P("section", "sp", None, None),
            P("section"),
            P("section"),
        ),
        out_specs=P("section", "sp", None),
        check_vma=False,
    )
```

```python
import functools
import math

import jax
import jax.numpy as jnp
from jax import lax
from jax.experimental import pallas as pl
from jax.experimental.pallas import tpu as pltpu
from jax.sharding import PartitionSpec as P

HEAD = 128
ROWS = 128
SIDE = 4
CACHE = 256
TILE = 512
SPAN = SIDE * SIDE * ROWS
ROPE_BASE = 500000.0
NEG = -1e30
SCALE = math.log2(math.e) / math.sqrt(HEAD)
MESH = pl.DeviceIdType.MESH
CONTRACT = (((1,), (1,)), ((), ()))
ORDER = (1, 3, 2)


def place(family, a, t):
    return SIDE * a + t if family == 0 else SIDE * t + a


def head_of(family, a):
    return 2 * a + 1 - a // 2 if family == 0 else 2 * a + a // 2


def kernel(
    sections,
    length_ref,
    query,
    keyval,
    cache,
    block_tab,
    row_tab,
    out,
    kvland,
    qland,
    cland,
    keys,
    values,
    qa,
    qb,
    sa,
    sb,
    ma,
    mb,
    obuf,
    kv1_send,
    kv2_send,
    kv_recv,
    q_send,
    q_recv,
    c_send,
    c_recv,
    o_send,
    o_recv,
):
    s = lax.axis_index("section")
    d = lax.axis_index("sp")
    x = d // SIDE
    y = d % SIDE
    head_at = (x, y)
    row_at = (y, x)
    after = lax.rem(s + 1, sections)
    before = lax.rem(s + sections - 1, sections)

    barrier = pltpu.get_barrier_semaphore()
    peers = []
    for k in range(1, SIDE):
        for f in range(2):
            peers.append((s, place(f, lax.rem(head_at[f] + k, SIDE), row_at[f])))
    for section in (after, before):
        peers.append((section, d))
        for k in range(1, SIDE):
            for f in range(2):
                peers.append((section, place(f, lax.rem(head_at[f] + k, SIDE), row_at[f])))
    for peer in peers:
        pl.semaphore_signal(barrier, inc=1, device_id=peer, device_id_type=MESH)
    pl.semaphore_wait(barrier, len(peers))

    def remote(source, target, send, recv, section, device):
        return pltpu.make_async_remote_copy(
            src_ref=source,
            dst_ref=target,
            send_sem=send,
            recv_sem=recv,
            device_id=(section, device),
            device_id_type=MESH,
        )

    def kv_part(f, a):
        return keyval.at[:, pl.ds(pl.multiple_of(head_of(f, a) * 256, 256), 256)]

    def q_part(f, a, half):
        return query.at[:, pl.ds(pl.multiple_of(head_of(f, a) * 1024 + half * 512, 512), 512)]

    def kv1(f, k):
        a = lax.rem(head_at[f] + k, SIDE)
        return remote(
            kv_part(f, a), kvland.at[f, d], kv1_send.at[f, k - 1], kv_recv.at[f, d], s, place(f, a, row_at[f])
        )

    def kv2(f, j, k):
        block = place(f, lax.rem(head_at[f] + j, SIDE), row_at[f])
        source = kv_part(f, head_at[f]) if j == 0 else kvland.at[f, block]
        target = place(f, head_at[f], lax.rem(row_at[f] + k, SIDE))
        return remote(source, kvland.at[f, block], kv2_send.at[f, j, k - 1], kv_recv.at[f, block], s, target)

    def q_copy(f, k, half):
        a = lax.rem(head_at[f] + k, SIDE)
        return remote(
            q_part(f, a, half),
            qland.at[f, head_at[f], half],
            q_send.at[f, k - 1, half],
            q_recv.at[f, head_at[f], half],
            s,
            place(f, a, row_at[f]),
        )

    def kv_own(f):
        return pltpu.make_async_copy(kv_part(f, head_at[f]), kvland.at[f, d], kv_recv.at[f, d])

    def q_own(f, half):
        return pltpu.make_async_copy(
            q_part(f, head_at[f], half), qland.at[f, head_at[f], half], q_recv.at[f, head_at[f], half]
        )

    def q_wait(f, a, half):
        pltpu.make_async_copy(q_part(f, a, half), qland.at[f, a, half], q_recv.at[f, a, half]).wait()

    def kv_wait(f, block):
        pltpu.make_async_copy(kv_part(f, 0), kvland.at[f, block], kv_recv.at[f, block]).wait()

    def cache_own(f):
        return pltpu.make_async_copy(cache, cland.at[f], c_recv.at[f])

    def cache_copy(f, k):
        if f == 0:
            target = SIDE * x + SIDE - 1 - y
        else:
            target = SIDE * lax.rem(x + k, SIDE) + y
        return remote(cache, cland.at[f], c_send.at[f, k - 1], c_recv.at[f], s, target)

    holds = (x // 2 != y // 2, x == y)

    def out_copy(f, a, half):
        column = head_of(f, head_at[f]) * 1024 + half * 512
        return remote(
            obuf.at[f, a, half],
            out.at[:, pl.ds(pl.multiple_of(column, 512), 512)],
            o_send.at[f, a, half],
            o_recv.at[f, head_at[f], half],
            after,
            place(f, a, row_at[f]),
        )

    def out_wait(f, a, half):
        column = head_of(f, a) * 1024 + half * 512
        pltpu.make_async_copy(
            obuf.at[f, a, half], out.at[:, pl.ds(pl.multiple_of(column, 512), 512)], o_recv.at[f, a, half]
        ).wait()

    def gather(f, j, act):
        for k in ORDER:
            if f == 0:
                act(kv2(f, j, k))
            else:

                @pl.when(row_at[f] + k < SIDE)
                def _(k=k):
                    act(kv2(f, j, k))

    def start(copy):
        copy.start()

    for k in ORDER:
        kv1(1, k).start()
    gather(1, 0, start)
    for half in range(2):
        for k in (3, 1, 2):
            q_copy(1, k, half).start()
    for f in (1, 0):
        kv_own(f).start()
        for half in range(2):
            q_own(f, half).start()

    @pl.when(holds[1])
    def _():
        cache_own(1).start()
        for k in ORDER:
            cache_copy(1, k).start()

    values[:, :, HEAD:] = jnp.ones((2, CACHE + SPAN, HEAD), jnp.bfloat16)

    def forward(f):
        for j in ORDER:
            kv_wait(f, place(f, lax.rem(head_at[f] + j, SIDE), row_at[f]))
            gather(f, j, start)

    forward(1)
    for k in ORDER:
        kv1(0, k).start()
    gather(0, 0, start)
    for half in range(2):
        for k in (3, 1, 2):
            q_copy(0, k, half).start()

    @pl.when(holds[0])
    def _():
        cache_own(0).start()
        cache_copy(0, 1).start()

    for f in (1, 0):
        kv_wait(f, d)

    def tables(block):
        cos_block = block_tab[0, block]
        sin_block = block_tab[1, block]
        cos_signed = block_tab[2, block]
        sin_signed = block_tab[3, block]
        cos_row = row_tab[0]
        sin_row = row_tab[1]
        cosine = cos_block * cos_row - sin_block * sin_row
        sine = sin_signed * cos_row + cos_signed * sin_row
        return cosine, sine

    def rotate(entries, cosine, sine):
        wide = entries.astype(jnp.float32)
        return wide * cosine + pltpu.roll(wide, HEAD // 2, 1) * sine

    def take_block(f, block):
        cosine, sine = tables(block)
        first = pl.multiple_of(CACHE + block * ROWS, ROWS)
        keys[f, pl.ds(first, ROWS), :] = rotate(kvland[f, block, :, :HEAD], cosine, sine).astype(jnp.bfloat16)
        values[f, pl.ds(first, ROWS), :HEAD] = kvland[f, block, :, HEAD:]

    def take_cache(f):
        cache_own(f).wait()
        keys[f, :CACHE, :] = cland[f, :, :HEAD]
        values[f, :CACHE, :HEAD] = cland[f, :, HEAD:]

    def take_query(f, a, half, target):
        q_wait(f, a, half)
        cosine, sine = tables(place(f, a, row_at[f]))
        for h in range(TILE // ROWS):
            head = qland[f, a, half, :, h * HEAD : (h + 1) * HEAD]
            target[h * ROWS : (h + 1) * ROWS, :] = (rotate(head, cosine, sine) * SCALE).astype(jnp.bfloat16)

    length = length_ref[0]

    def score(f, q_ref, reach, shift, s_ref, m_ref):
        q = q_ref[...]
        column = lax.broadcasted_iota(jnp.int32, (1, CACHE), 1)
        part = lax.dot_general(q, keys[f, :CACHE, :], CONTRACT, preferred_element_type=jnp.float32)
        part = jnp.where(column < length, part, NEG)
        s_ref[:, :CACHE] = part
        top = jnp.maximum(part[:, :128], part[:, 128:])
        if reach > 512:
            part = lax.dot_general(
                q, keys[f, CACHE : reach - 256, :], CONTRACT, preferred_element_type=jnp.float32
            )
            s_ref[:, CACHE : reach - 256] = part
            for c in range(0, reach - 512, 128):
                top = jnp.maximum(top, part[:, c : c + 128])
        part = lax.dot_general(
            q, keys[f, reach - 256 : reach + 256, :], CONTRACT, preferred_element_type=jnp.float32
        )
        column = lax.broadcasted_iota(jnp.int32, (1, 512), 1)
        row = lax.rem(lax.broadcasted_iota(jnp.int32, (TILE, 1), 0), ROWS) + shift
        part = jnp.where(column <= row, part, NEG)
        s_ref[:, reach - 256 : reach + 256] = part
        for c in range(0, 512, 128):
            top = jnp.maximum(top, part[:, c : c + 128])
        m_ref[...] = jnp.broadcast_to(jnp.max(top, axis=1, keepdims=True), (TILE, 128))

    def combine(f, a, half, reach, s_ref, m_ref):
        width = reach + CACHE
        top = jnp.concatenate([m_ref[...]] * (width // 128), axis=1)
        probs = jnp.exp2(s_ref[:, :width] - top).astype(jnp.bfloat16)
        mixed = jnp.dot(probs, values[f, :width, :], preferred_element_type=jnp.float32)
        result = (mixed[:, :HEAD] / mixed[:, HEAD:]).astype(jnp.bfloat16)
        for h in range(TILE // ROWS):
            obuf[f, a, half, :, h * HEAD : (h + 1) * HEAD] = result[h * ROWS : (h + 1) * ROWS, :]

    def take_column(k):
        def one(a, carry):
            block = place(1, a, lax.rem(row_at[1] + k, SIDE))
            if k:
                kv_wait(1, block)
            take_block(1, block)
            return carry

        lax.fori_loop(0, SIDE, one, 0)

    take_column(0)
    for k in ORDER:

        @pl.when(row_at[1] + k >= SIDE)
        def _(k=k):
            take_column(k)

    take_cache(1)

    def turn(f, n):
        n = jnp.int32(n)
        step = n + (n == 2).astype(jnp.int32) - (n == 3).astype(jnp.int32)
        return lax.rem(head_at[f] + step, SIDE)

    def run(reach):
        def at(n):
            return turn(1, n)

        take_query(1, at(0), 0, qa)
        score(1, qa, reach, at(0) * ROWS, sa, ma)

        def unit(n, carry):
            take_query(1, at(n), 1, qb)
            score(1, qb, reach, at(n) * ROWS, sb, mb)
            combine(1, at(n), 0, reach, sa, ma)

            @pl.when(n == 0)
            def _():
                forward(0)

            @pl.when(n > 0)
            def _():
                out_copy(1, at(n - 1), 1).start()

            @pl.when(n < SIDE - 1)
            def _():
                take_query(1, at(n + 1), 0, qa)
                score(1, qa, reach, at(n + 1) * ROWS, sa, ma)
                combine(1, at(n), 1, reach, sb, mb)

            @pl.when(n == SIDE - 1)
            def _():
                combine(1, at(n), 1, reach, sb, mb)

            out_copy(1, at(n), 0).start()
            return carry

        lax.fori_loop(0, SIDE, unit, 0)

    for t in range(SIDE):

        @pl.when(row_at[1] == t)
        def _(t=t):
            run(512 * (t + 1))

    shift = row_at[0] * ROWS
    take_cache(0)

    def take_piece(a, carry):
        for k in ORDER:
            kv_wait(0, place(0, a, lax.rem(row_at[0] + k, SIDE)))
        for t in range(SIDE):
            take_block(0, place(0, a, t))
        return carry

    lax.fori_loop(0, SIDE, take_piece, 0)
    take_query(0, lax.rem(x + 1, SIDE), 0, qa)
    for i in range(SIDE):

        @pl.when(lax.rem(x + 1, SIDE) == i)
        def _(i=i):
            score(0, qa, 512 * (i + 1), shift, sa, ma)

    out_copy(1, turn(1, jnp.int32(3)), 1).start()

    def unit0(n, carry):
        now = lax.rem(x + 1 + n, SIDE)
        then = lax.rem(now + 1, SIDE)
        take_query(0, now, 1, qb)

        @pl.when(n < SIDE - 1)
        def _():
            take_query(0, then, 0, qa)

        for i in range(SIDE):

            @pl.when(now == i)
            def _(i=i):
                reach = 512 * (i + 1)
                score(0, qb, reach, shift, sb, mb)
                combine(0, i, 0, reach, sa, ma)

        @pl.when(n > 0)
        def _():
            out_copy(0, lax.rem(now + SIDE - 1, SIDE), 1).start()

        for i in range(SIDE):

            @pl.when(jnp.logical_and(now == i, n < SIDE - 1))
            def _(i=i):
                score(0, qa, 512 * ((i + 1) % SIDE + 1), shift, sa, ma)
                combine(0, i, 1, 512 * (i + 1), sb, mb)

            @pl.when(jnp.logical_and(now == i, n == SIDE - 1))
            def _(i=i):
                combine(0, i, 1, 512 * (i + 1), sb, mb)

        out_copy(0, now, 0).start()
        return carry

    lax.fori_loop(0, SIDE, unit0, 0)
    out_copy(0, x, 1).start()

    def drain(copy):
        copy.wait_send()

    for f in range(2):
        for k in ORDER:
            kv1(f, k).wait_send()
            for half in range(2):
                q_copy(f, k, half).wait_send()
        for j in range(SIDE):
            gather(f, j, drain)
    for f, ks in ((0, (1,)), (1, ORDER)):

        @pl.when(holds[f])
        def _(f=f, ks=ks):
            for k in ks:
                cache_copy(f, k).wait_send()

    for f in range(2):
        for a in range(SIDE):
            for half in range(2):
                out_copy(f, a, half).wait_send()
                out_wait(f, a, half)


def angles(positions):
    exponent = jnp.arange(HEAD // 2, dtype=jnp.float32) * (-2.0 / HEAD)
    frequency = jnp.power(jnp.float32(ROPE_BASE), exponent)
    angle = positions.astype(jnp.float32)[:, None] * frequency[None, :]
    return jnp.cos(angle), jnp.sin(angle)


def on_device(query, keyval, cache, offsets, lengths):
    sections = lax.axis_size("section")
    blocks = offsets[0] + ROWS * jnp.arange(SIDE * SIDE, dtype=jnp.int32)
    cos_block, sin_block = angles(blocks)
    cos_row, sin_row = angles(jnp.arange(ROWS, dtype=jnp.int32))
    block_tab = jnp.stack(
        [
            jnp.concatenate([cos_block, cos_block], axis=1),
            jnp.concatenate([sin_block, sin_block], axis=1),
            jnp.concatenate([-cos_block, cos_block], axis=1),
            jnp.concatenate([-sin_block, sin_block], axis=1),
        ]
    )[:, :, None, :]
    row_tab = jnp.stack(
        [
            jnp.concatenate([cos_row, cos_row], axis=1),
            jnp.concatenate([sin_row, sin_row], axis=1),
        ]
    )
    bf16 = jnp.bfloat16
    anywhere = pl.BlockSpec(memory_space=pl.ANY)
    far = pl.BlockSpec(memory_space=pltpu.HBM)
    vmem = pl.BlockSpec(memory_space=pltpu.VMEM)
    result = pl.pallas_call(
        functools.partial(kernel, sections),
        out_shape=jax.ShapeDtypeStruct((ROWS, 64 * HEAD), bf16),
        in_specs=[pl.BlockSpec(memory_space=pltpu.SMEM), far, far, far, vmem, vmem],
        out_specs=anywhere,
        scratch_shapes=[
            pltpu.VMEM((2, SIDE * SIDE, ROWS, 2 * HEAD), bf16),
            pltpu.VMEM((2, SIDE, 2, ROWS, TILE), bf16),
            pltpu.VMEM((2, CACHE, 2 * HEAD), bf16),
            pltpu.VMEM((2, CACHE + SPAN, HEAD), bf16),
            pltpu.VMEM((2, CACHE + SPAN, 2 * HEAD), bf16),
            pltpu.VMEM((TILE, HEAD), bf16),
            pltpu.VMEM((TILE, HEAD), bf16),
            pltpu.VMEM((TILE, CACHE + SPAN), jnp.float32),
            pltpu.VMEM((TILE, CACHE + SPAN), jnp.float32),
            pltpu.VMEM((TILE, 128), jnp.float32),
            pltpu.VMEM((TILE, 128), jnp.float32),
            pltpu.VMEM((2, SIDE, 2, ROWS, TILE), bf16),
            pltpu.SemaphoreType.DMA((2, 3)),
            pltpu.SemaphoreType.DMA((2, SIDE, 3)),
            pltpu.SemaphoreType.DMA((2, SIDE * SIDE)),
            pltpu.SemaphoreType.DMA((2, 3, 2)),
            pltpu.SemaphoreType.DMA((2, SIDE, 2)),
            pltpu.SemaphoreType.DMA((2, 3)),
            pltpu.SemaphoreType.DMA((2,)),
            pltpu.SemaphoreType.DMA((2, SIDE, 2)),
            pltpu.SemaphoreType.DMA((2, SIDE, 2)),
        ],
        compiler_params=pltpu.CompilerParams(
            collective_id=0, has_side_effects=True, vmem_limit_bytes=48 << 20
        ),
    )(lengths, *(pltpu.with_memory_space_constraint(z, pltpu.HBM) for z in (query[0], keyval[0], cache[0, 0])), block_tab, row_tab)
    return result[None]


def solution(mesh):
    return jax.shard_map(
        on_device,
        mesh=mesh,
        in_specs=(
            P("section", "sp", None),
            P("section", "sp", None),
            P("section", "sp", None, None),
            P("section"),
            P("section"),
        ),
        out_specs=P("section", "sp", None),
        check_vma=False,
    )
```

```python
import functools
import math

import jax
import jax.numpy as jnp
from jax import lax
from jax.experimental import pallas as pl
from jax.experimental.pallas import tpu as pltpu
from jax.sharding import PartitionSpec as P

HEAD = 128
ROWS = 128
SIDE = 4
CACHE = 256
TILE = 512
SPAN = SIDE * SIDE * ROWS
ROPE_BASE = 500000.0
NEG = -1e30
SCALE = math.log2(math.e) / math.sqrt(HEAD)
MESH = pl.DeviceIdType.MESH
CONTRACT = (((1,), (1,)), ((), ()))
ORDER = (2, 1, 3)


def place(family, a, t):
    return SIDE * a + t if family == 0 else SIDE * t + a


def head_of(family, a):
    return 2 * a + 1 - a // 2 if family == 0 else 2 * a + a // 2


def kernel(
    sections,
    length_ref,
    query,
    keyval,
    cache,
    block_tab,
    row_tab,
    out,
    kvland,
    qland,
    cland,
    keys,
    values,
    qa,
    qb,
    sa,
    sb,
    ma,
    mb,
    obuf,
    kv1_send,
    kv2_send,
    kv_recv,
    q_send,
    q_recv,
    c_send,
    c_recv,
    o_send,
    o_recv,
):
    s = lax.axis_index("section")
    d = lax.axis_index("sp")
    x = d // SIDE
    y = d % SIDE
    head_at = (x, y)
    row_at = (y, x)
    after = lax.rem(s + 1, sections)
    before = lax.rem(s + sections - 1, sections)

    barrier = pltpu.get_barrier_semaphore()
    peers = []
    for k in range(1, SIDE):
        for f in range(2):
            peers.append((s, place(f, lax.rem(head_at[f] + k, SIDE), row_at[f])))
    for section in (after, before):
        peers.append((section, d))
        for k in range(1, SIDE):
            for f in range(2):
                peers.append((section, place(f, lax.rem(head_at[f] + k, SIDE), row_at[f])))
    for peer in peers:
        pl.semaphore_signal(barrier, inc=1, device_id=peer, device_id_type=MESH)
    pl.semaphore_wait(barrier, len(peers))

    def remote(source, target, send, recv, section, device):
        return pltpu.make_async_remote_copy(
            src_ref=source,
            dst_ref=target,
            send_sem=send,
            recv_sem=recv,
            device_id=(section, device),
            device_id_type=MESH,
        )

    def kv_part(f, a):
        return keyval.at[:, pl.ds(pl.multiple_of(head_of(f, a) * 256, 256), 256)]

    def q_part(f, a, half):
        return query.at[:, pl.ds(pl.multiple_of(head_of(f, a) * 1024 + half * 512, 512), 512)]

    def kv1(f, k):
        a = lax.rem(head_at[f] + k, SIDE)
        return remote(
            kv_part(f, a), kvland.at[f, d], kv1_send.at[f, k - 1], kv_recv.at[f, d], s, place(f, a, row_at[f])
        )

    def kv2(f, j, k):
        block = place(f, lax.rem(head_at[f] + j, SIDE), row_at[f])
        source = kv_part(f, head_at[f]) if j == 0 else kvland.at[f, block]
        target = place(f, head_at[f], lax.rem(row_at[f] + k, SIDE))
        return remote(source, kvland.at[f, block], kv2_send.at[f, j, k - 1], kv_recv.at[f, block], s, target)

    def q_copy(f, k, half):
        a = lax.rem(head_at[f] + k, SIDE)
        return remote(
            q_part(f, a, half),
            qland.at[f, head_at[f], half],
            q_send.at[f, k - 1, half],
            q_recv.at[f, head_at[f], half],
            s,
            place(f, a, row_at[f]),
        )

    def kv_own(f):
        return pltpu.make_async_copy(kv_part(f, head_at[f]), kvland.at[f, d], kv_recv.at[f, d])

    def q_own(f, half):
        return pltpu.make_async_copy(
            q_part(f, head_at[f], half), qland.at[f, head_at[f], half], q_recv.at[f, head_at[f], half]
        )

    def q_wait(f, a, half):
        pltpu.make_async_copy(q_part(f, a, half), qland.at[f, a, half], q_recv.at[f, a, half]).wait()

    def kv_wait(f, block):
        pltpu.make_async_copy(kv_part(f, 0), kvland.at[f, block], kv_recv.at[f, block]).wait()

    def cache_own(f):
        return pltpu.make_async_copy(cache, cland.at[f], c_recv.at[f])

    def cache_copy(f, k):
        if f == 0:
            target = SIDE * x + SIDE - 1 - y
        else:
            target = SIDE * lax.rem(x + k, SIDE) + y
        return remote(cache, cland.at[f], c_send.at[f, k - 1], c_recv.at[f], s, target)

    holds = (x // 2 != y // 2, x == y)

    def out_copy(f, a, half):
        column = head_of(f, head_at[f]) * 1024 + half * 512
        return remote(
            obuf.at[f, a, half],
            out.at[:, pl.ds(pl.multiple_of(column, 512), 512)],
            o_send.at[f, a, half],
            o_recv.at[f, head_at[f], half],
            after,
            place(f, a, row_at[f]),
        )

    def out_wait(f, a, half):
        column = head_of(f, a) * 1024 + half * 512
        pltpu.make_async_copy(
            obuf.at[f, a, half], out.at[:, pl.ds(pl.multiple_of(column, 512), 512)], o_recv.at[f, a, half]
        ).wait()

    def gather(f, j, act):
        for k in ORDER:
            if f == 0:

                @pl.when(jnp.logical_or(lax.rem(x + j, SIDE) < SIDE - 1, y + k < SIDE))
                def _(k=k):
                    act(kv2(f, j, k))

            else:

                @pl.when(row_at[f] + k < SIDE)
                def _(k=k):
                    act(kv2(f, j, k))

    def start(copy):
        copy.start()

    for k in ORDER:
        kv1(1, k).start()
    gather(1, 0, start)
    for half in range(2):
        for k in (3, 1, 2):
            q_copy(1, k, half).start()
    for f in (1, 0):
        kv_own(f).start()
        for half in range(2):
            q_own(f, half).start()

    @pl.when(holds[1])
    def _():
        cache_own(1).start()
        for k in ORDER:
            cache_copy(1, k).start()

    values[:, :, HEAD:] = jnp.ones((2, CACHE + SPAN, HEAD), jnp.bfloat16)
    last = CACHE + SPAN - 512
    values[0, last:, :HEAD] = jnp.zeros((512, HEAD), jnp.bfloat16)
    keys[0, last:, :] = jnp.zeros((512, HEAD), jnp.bfloat16)

    def forward(f):
        for j in ORDER:
            kv_wait(f, place(f, lax.rem(head_at[f] + j, SIDE), row_at[f]))
            gather(f, j, start)

    forward(1)
    for k in ORDER:
        kv1(0, k).start()
    gather(0, 0, start)
    for half in range(2):
        for k in (3, 1, 2):
            q_copy(0, k, half).start()

    @pl.when(holds[0])
    def _():
        cache_own(0).start()
        cache_copy(0, 1).start()

    for f in (1, 0):
        kv_wait(f, d)

    def tables(block):
        cos_block = block_tab[0, block]
        sin_block = block_tab[1, block]
        cos_signed = block_tab[2, block]
        sin_signed = block_tab[3, block]
        cos_row = row_tab[0]
        sin_row = row_tab[1]
        cosine = cos_block * cos_row - sin_block * sin_row
        sine = sin_signed * cos_row + cos_signed * sin_row
        return cosine, sine

    def rotate(entries, cosine, sine):
        wide = entries.astype(jnp.float32)
        return wide * cosine + pltpu.roll(wide, HEAD // 2, 1) * sine

    def take_block(f, block):
        cosine, sine = tables(block)
        first = pl.multiple_of(CACHE + block * ROWS, ROWS)
        keys[f, pl.ds(first, ROWS), :] = rotate(kvland[f, block, :, :HEAD], cosine, sine).astype(jnp.bfloat16)
        values[f, pl.ds(first, ROWS), :HEAD] = kvland[f, block, :, HEAD:]

    def take_cache(f):
        cache_own(f).wait()
        keys[f, :CACHE, :] = cland[f, :, :HEAD]
        values[f, :CACHE, :HEAD] = cland[f, :, HEAD:]

    def take_query(f, a, half, target):
        q_wait(f, a, half)
        cosine, sine = tables(place(f, a, row_at[f]))
        for h in range(TILE // ROWS):
            head = qland[f, a, half, :, h * HEAD : (h + 1) * HEAD]
            target[h * ROWS : (h + 1) * ROWS, :] = (rotate(head, cosine, sine) * SCALE).astype(jnp.bfloat16)

    length = length_ref[0]

    def score(f, q_ref, reach, shift, s_ref, m_ref):
        q = q_ref[...]
        column = lax.broadcasted_iota(jnp.int32, (1, CACHE), 1)
        part = lax.dot_general(q, keys[f, :CACHE, :], CONTRACT, preferred_element_type=jnp.float32)
        part = jnp.where(column < length, part, NEG)
        s_ref[:, :CACHE] = part
        top = jnp.maximum(part[:, :128], part[:, 128:])
        if reach > 512:
            part = lax.dot_general(
                q, keys[f, CACHE : reach - 256, :], CONTRACT, preferred_element_type=jnp.float32
            )
            s_ref[:, CACHE : reach - 256] = part
            for c in range(0, reach - 512, 128):
                top = jnp.maximum(top, part[:, c : c + 128])
        part = lax.dot_general(
            q, keys[f, reach - 256 : reach + 256, :], CONTRACT, preferred_element_type=jnp.float32
        )
        column = lax.broadcasted_iota(jnp.int32, (1, 512), 1)
        row = lax.rem(lax.broadcasted_iota(jnp.int32, (TILE, 1), 0), ROWS) + shift
        part = jnp.where(column <= row, part, NEG)
        s_ref[:, reach - 256 : reach + 256] = part
        for c in range(0, 512, 128):
            top = jnp.maximum(top, part[:, c : c + 128])
        m_ref[...] = jnp.broadcast_to(jnp.max(top, axis=1, keepdims=True), (TILE, 128))

    def combine(f, a, half, reach, s_ref, m_ref):
        width = reach + CACHE
        top = jnp.concatenate([m_ref[...]] * (width // 128), axis=1)
        probs = jnp.exp2(s_ref[:, :width] - top).astype(jnp.bfloat16)
        mixed = jnp.dot(probs, values[f, :width, :], preferred_element_type=jnp.float32)
        result = (mixed[:, :HEAD] / mixed[:, HEAD:]).astype(jnp.bfloat16)
        for h in range(TILE // ROWS):
            obuf[f, a, half, :, h * HEAD : (h + 1) * HEAD] = result[h * ROWS : (h + 1) * ROWS, :]

    def take_column(k):
        def one(a, carry):
            block = place(1, a, lax.rem(row_at[1] + k, SIDE))
            if k:
                kv_wait(1, block)
            take_block(1, block)
            return carry

        lax.fori_loop(0, SIDE, one, 0)

    take_column(0)
    for k in ORDER:

        @pl.when(row_at[1] + k >= SIDE)
        def _(k=k):
            take_column(k)

    take_cache(1)

    def turn(f, n):
        n = jnp.int32(n)
        step = n + (n == 2).astype(jnp.int32) - (n == 3).astype(jnp.int32)
        return lax.rem(head_at[f] + step, SIDE)

    def run(reach):
        def at(n):
            return turn(1, n)

        take_query(1, at(0), 0, qa)
        score(1, qa, reach, at(0) * ROWS, sa, ma)

        def unit(n, carry):
            take_query(1, at(n), 1, qb)
            score(1, qb, reach, at(n) * ROWS, sb, mb)
            combine(1, at(n), 0, reach, sa, ma)

            @pl.when(n == 0)
            def _():
                forward(0)

            @pl.when(n > 0)
            def _():
                out_copy(1, at(n - 1), 1).start()

            @pl.when(n < SIDE - 1)
            def _():
                take_query(1, at(n + 1), 0, qa)
                score(1, qa, reach, at(n + 1) * ROWS, sa, ma)
                combine(1, at(n), 1, reach, sb, mb)

            @pl.when(n == SIDE - 1)
            def _():
                combine(1, at(n), 1, reach, sb, mb)

            out_copy(1, at(n), 0).start()
            return carry

        lax.fori_loop(0, SIDE, unit, 0)

    for t in range(SIDE):

        @pl.when(row_at[1] == t)
        def _(t=t):
            run(512 * (t + 1))

    shift = row_at[0] * ROWS
    take_cache(0)

    def take_piece(a, carry):
        for k in ORDER:

            @pl.when(jnp.logical_or(a < SIDE - 1, y + k >= SIDE))
            def _(k=k):
                kv_wait(0, place(0, a, lax.rem(y + k, SIDE)))

        for t in range(SIDE):

            @pl.when(jnp.logical_or(a < SIDE - 1, t <= y))
            def _(t=t):
                take_block(0, place(0, a, t))

        return carry

    first = lax.rem(x + 1, SIDE)
    lax.fori_loop(0, first + 1, take_piece, 0)
    take_query(0, first, 0, qa)
    for i in range(SIDE):

        @pl.when(lax.rem(x + 1, SIDE) == i)
        def _(i=i):
            score(0, qa, 512 * (i + 1), shift, sa, ma)

    out_copy(1, turn(1, jnp.int32(3)), 1).start()

    def unit0(n, carry):
        now = lax.rem(x + 1 + n, SIDE)
        then = lax.rem(now + 1, SIDE)
        take_query(0, now, 1, qb)

        for i in range(SIDE):

            @pl.when(now == i)
            def _(i=i):
                reach = 512 * (i + 1)
                score(0, qb, reach, shift, sb, mb)
                combine(0, i, 0, reach, sa, ma)

        @pl.when(jnp.logical_and(n < SIDE - 1, then > first))
        def _():
            take_piece(then, 0)

        @pl.when(n < SIDE - 1)
        def _():
            take_query(0, then, 0, qa)

        @pl.when(n > 0)
        def _():
            out_copy(0, lax.rem(now + SIDE - 1, SIDE), 1).start()

        for i in range(SIDE):

            @pl.when(jnp.logical_and(now == i, n < SIDE - 1))
            def _(i=i):
                score(0, qa, 512 * ((i + 1) % SIDE + 1), shift, sa, ma)
                combine(0, i, 1, 512 * (i + 1), sb, mb)

            @pl.when(jnp.logical_and(now == i, n == SIDE - 1))
            def _(i=i):
                combine(0, i, 1, 512 * (i + 1), sb, mb)

        out_copy(0, now, 0).start()
        return carry

    lax.fori_loop(0, SIDE, unit0, 0)
    out_copy(0, x, 1).start()

    def drain(copy):
        copy.wait_send()

    for f in range(2):
        for k in ORDER:
            kv1(f, k).wait_send()
            for half in range(2):
                q_copy(f, k, half).wait_send()
        for j in range(SIDE):
            gather(f, j, drain)
    for f, ks in ((0, (1,)), (1, ORDER)):

        @pl.when(holds[f])
        def _(f=f, ks=ks):
            for k in ks:
                cache_copy(f, k).wait_send()

    for f in range(2):
        for a in range(SIDE):
            for half in range(2):
                out_copy(f, a, half).wait_send()
                out_wait(f, a, half)


def angles(positions):
    exponent = jnp.arange(HEAD // 2, dtype=jnp.float32) * (-2.0 / HEAD)
    frequency = jnp.power(jnp.float32(ROPE_BASE), exponent)
    angle = positions.astype(jnp.float32)[:, None] * frequency[None, :]
    return jnp.cos(angle), jnp.sin(angle)


def on_device(query, keyval, cache, offsets, lengths):
    sections = lax.axis_size("section")
    blocks = offsets[0] + ROWS * jnp.arange(SIDE * SIDE, dtype=jnp.int32)
    cos_block, sin_block = angles(blocks)
    cos_row, sin_row = angles(jnp.arange(ROWS, dtype=jnp.int32))
    block_tab = jnp.stack(
        [
            jnp.concatenate([cos_block, cos_block], axis=1),
            jnp.concatenate([sin_block, sin_block], axis=1),
            jnp.concatenate([-cos_block, cos_block], axis=1),
            jnp.concatenate([-sin_block, sin_block], axis=1),
        ]
    )[:, :, None, :]
    row_tab = jnp.stack(
        [
            jnp.concatenate([cos_row, cos_row], axis=1),
            jnp.concatenate([sin_row, sin_row], axis=1),
        ]
    )
    bf16 = jnp.bfloat16
    anywhere = pl.BlockSpec(memory_space=pl.ANY)
    far = pl.BlockSpec(memory_space=pltpu.HBM)
    vmem = pl.BlockSpec(memory_space=pltpu.VMEM)
    result = pl.pallas_call(
        functools.partial(kernel, sections),
        out_shape=jax.ShapeDtypeStruct((ROWS, 64 * HEAD), bf16),
        in_specs=[pl.BlockSpec(memory_space=pltpu.SMEM), far, far, far, vmem, vmem],
        out_specs=anywhere,
        scratch_shapes=[
            pltpu.VMEM((2, SIDE * SIDE, ROWS, 2 * HEAD), bf16),
            pltpu.VMEM((2, SIDE, 2, ROWS, TILE), bf16),
            pltpu.VMEM((2, CACHE, 2 * HEAD), bf16),
            pltpu.VMEM((2, CACHE + SPAN, HEAD), bf16),
            pltpu.VMEM((2, CACHE + SPAN, 2 * HEAD), bf16),
            pltpu.VMEM((TILE, HEAD), bf16),
            pltpu.VMEM((TILE, HEAD), bf16),
            pltpu.VMEM((TILE, CACHE + SPAN), jnp.float32),
            pltpu.VMEM((TILE, CACHE + SPAN), jnp.float32),
            pltpu.VMEM((TILE, 128), jnp.float32),
            pltpu.VMEM((TILE, 128), jnp.float32),
            pltpu.VMEM((2, SIDE, 2, ROWS, TILE), bf16),
            pltpu.SemaphoreType.DMA((2, 3)),
            pltpu.SemaphoreType.DMA((2, SIDE, 3)),
            pltpu.SemaphoreType.DMA((2, SIDE * SIDE)),
            pltpu.SemaphoreType.DMA((2, 3, 2)),
            pltpu.SemaphoreType.DMA((2, SIDE, 2)),
            pltpu.SemaphoreType.DMA((2, 3)),
            pltpu.SemaphoreType.DMA((2,)),
            pltpu.SemaphoreType.DMA((2, SIDE, 2)),
            pltpu.SemaphoreType.DMA((2, SIDE, 2)),
        ],
        compiler_params=pltpu.CompilerParams(
            collective_id=0, has_side_effects=True, vmem_limit_bytes=48 << 20
        ),
    )(lengths, *(pltpu.with_memory_space_constraint(z, pltpu.HBM) for z in (query[0], keyval[0], cache[0, 0])), block_tab, row_tab)
    return result[None]


def solution(mesh):
    return jax.shard_map(
        on_device,
        mesh=mesh,
        in_specs=(
            P("section", "sp", None),
            P("section", "sp", None),
            P("section", "sp", None, None),
            P("section"),
            P("section"),
        ),
        out_specs=P("section", "sp", None),
        check_vma=False,
    )
```
